128 devices in a mesh: rows: 64 (over x, y_lo, z, core), rep: 2 (over y_hi).
Axes of the slice: x: 4, y: 4 (y_hi: 2, y_lo: 2; y = y_hi * 2 + y_lo), z: 4, core: 2. Of those that a mesh axis runs over, the one named last changes fastest.
Arguments:
- features: bfloat16 [65536, 128], P(('rows', 'rep')), may hold values from -6 to 6
- weight: bfloat16 [128, 256], replicated, may hold values from -0.5 to 0.5
- shift_bias: float32 [256], replicated, may hold values from -3 to 3
- norm_gain: float32 [256], replicated, may hold values from 0.25 to 1.75
- tile_values: bfloat16 [512, 2, 88, 128, 128], P('rows', 'rep'), as said below
- tile_cols: int32 [512, 2, 88], P('rows', 'rep'), may hold values from 0 to 255, all different within a row
- tile_counts: int32 [512, 2], P('rows', 'rep'), may hold values from 1 to 88, as said below
- block_order: int32 [2, 256], replicated, may hold values from 0 to 255, each once within a row
Outputs:
- node_out: bfloat16 [65536, 256], P(('rows', 'rep'))
The draws below stay inside these ranges and needn't reach their ends.
Inputs may be any that keep to these rules, and one draw needn't show every extreme that they name: Slots 0 to tile_counts - 1 of a row block and column set are live, the rest are ignored; the largest count is reached. `tile_values`: tile entries are nonnegative.
All inputs are finite; a program needn't handle non-finite values.
Results may differ from the reference program's by a relative error of at most 0.0052.
Values may be sent and summed in bfloat16 or wider, within the bound.
No kernel may reach another device: no remote copies, remote signals or barrier semaphores. Data moves between devices by JAX's collectives and lax.ppermute only.
A program may use at most 192 MiB of HBM per device.

```python
import math
import jax
import jax.numpy as jnp
from jax import lax

F = 128
H = 256
BLK = 128
RB_DEV = 8
NBLK = 512
NSET = 256
KR = 88
NODES = 65536
N_ROWS = 64
N_REP = 2


def draw_tile_values(key, part):
    shape = (NBLK, N_REP, KR, BLK, BLK)
    scale = 1.0 / math.sqrt(BLK * KR // 2)
    values = jnp.abs(jax.random.normal(key, shape, jnp.float32)) * scale
    return values.astype(jnp.bfloat16)


def draw_tile_counts(key, part):
    key_heavy, key_high, key_low, key_spot = jax.random.split(key, 4)
    heavy = jax.random.randint(key_heavy, (NBLK, N_REP), 0, 4) == 0
    high_counts = jax.random.randint(key_high, (NBLK, N_REP), KR // 2, KR + 1)
    low_counts = jax.random.randint(key_low, (NBLK, N_REP), 1, KR // 2 + 1)
    values = jnp.where(heavy, high_counts, low_counts).reshape(-1)
    spot = jax.random.randint(key_spot, (), 0, NBLK * N_REP)
    values = jnp.where(jnp.arange(NBLK * N_REP) == spot, KR, values)
    return values.reshape(NBLK, N_REP).astype(jnp.int32)


def levels(rng, shape, cuts, least, top_value):
    factor_of, own = 1.0, jax.random.fold_in(rng, 6)
    for dim, shards_of in cuts:
        heights = jnp.exp(jax.random.uniform(jax.random.fold_in(own, dim), (shards_of,), jnp.float32, least / len(cuts), top_value / len(cuts)))
        factor_of = factor_of * jnp.repeat(heights, shape[dim] // shards_of).reshape([-1 if axis == dim else 1 for axis in range(len(shape))])
    return factor_of


def choose_distinct(rng, rows, number_of, top, lift):
    ranking = jax.random.permutation(jax.random.fold_in(rng, 1), number_of)
    favour = ranking
    for power in range(3):
        favour = favour * favour // number_of
    favour = favour * lift // number_of
    chance = jax.random.randint(jax.random.fold_in(rng, 2), (rows, number_of), 0, 4096) + favour
    fixed_rows = jax.random.permutation(jax.random.fold_in(rng, 3), rows)[jnp.arange(number_of) % rows]
    chance = jnp.where(jnp.arange(rows)[:, None] == fixed_rows[None, :], 1 << 14, chance)
    priority = chance * number_of + jnp.arange(number_of)
    return lax.top_k(priority.astype(jnp.int32), top)[1].astype(jnp.int32)


def normal_values(rng, shape, spread, bound, cuts=(), dtype=jnp.bfloat16):
    drawn = jax.random.normal(rng, shape, jnp.float32) * spread
    if len(cuts) > 0:
        drawn = levels(rng, shape, cuts, -0.22, 0.18) * drawn
    return jnp.clip(drawn, min=-bound, max=bound).astype(dtype)


def setup_inputs(seed: int = 0) -> dict:
    splits = jax.random.split(jax.random.key(seed), 9)
    return {
        "features": normal_values(splits[0], (NODES, F), 1.0, 6.0, ((0, 128),)),
        "weight": normal_values(splits[1], (F, H), F ** -0.5, 0.5),
        "shift_bias": normal_values(splits[2], (H,), 0.5, 3.0, (), jnp.float32),
        "norm_gain": jnp.clip(1.0 + 0.15 * jax.random.normal(splits[3], (H,), jnp.float32), 0.25, 1.75),
        "tile_values": draw_tile_values(jax.random.fold_in(splits[8], 71), 0),
        "tile_cols": choose_distinct(splits[5], NBLK * N_REP, NSET, KR, 0).reshape((NBLK, N_REP, KR)),
        "tile_counts": draw_tile_counts(jax.random.fold_in(splits[8], 71), 0),
        "block_order": jax.vmap(lambda own: jax.random.permutation(own, NSET))(jax.random.split(splits[7], N_REP)).reshape((N_REP, NSET)).astype(jnp.int32),
    }


def reference(features, weight, shift_bias, norm_gain, tile_values, tile_cols, tile_counts, block_order):
    projected = jnp.dot(features, weight, preferred_element_type=jnp.float32).astype(jnp.bfloat16)
    half_owner = RB_DEV // N_REP
    column_sets = projected.reshape(N_ROWS, N_REP, half_owner, BLK, H)
    column_sets = jnp.transpose(column_sets, (1, 0, 2, 3, 4)).reshape(N_REP, NSET, BLK, H)

    def one_block(inputs):
        block_tiles, block_cols, block_counts = inputs
        running = jnp.zeros((BLK, H), jnp.float32)
        for replica in range(N_REP):
            positions = block_order[replica][block_cols[replica]]
            picked_rows = column_sets[replica][positions].astype(jnp.float32)
            live_mask = jnp.arange(KR) < block_counts[replica]
            picked_rows = jnp.where(live_mask[:, None, None], picked_rows, jnp.float32(0.0))
            running = running + jnp.einsum('kij,kjh->ih', block_tiles[replica].astype(jnp.float32), picked_rows)
        return running
    summed = lax.map(one_block, (tile_values, tile_cols, tile_counts))
    hidden = jnp.maximum(summed.reshape(NODES, H) + shift_bias, 0.0)
    row_mean = lax.optimization_barrier(jnp.mean(hidden, axis=1, keepdims=True))
    centered = hidden - row_mean
    row_var = lax.optimization_barrier(jnp.mean(centered * centered, axis=1, keepdims=True))
    return (centered / jnp.sqrt(row_var + 1e-05) * norm_gain).astype(jnp.bfloat16)
```

```python
import jax
import jax.numpy as jnp
from jax import lax
from jax.experimental import pallas as pl
from jax.experimental.pallas import tpu as pltpu
from jax.sharding import PartitionSpec as P

AXES = ("rows", "rep")
NX, NY, NZ, NC, NR = 4, 2, 4, 2, 2
GROUP = 8


def place(g):
    rep = g % NR
    i = g // NR
    return i // (NY * NZ * NC), i // (NZ * NC) % NY, i // NC % NZ, i % NC, rep


def index(x, y, z, core, rep):
    return ((((x % NX) * NY + y) * NZ + z % NZ) * NC + core) * NR + rep


def pairs(move):
    return [(g, index(*move(*place(g)))) for g in range(NX * NY * NZ * NC * NR)]


def first(s):
    return pairs(lambda x, y, z, c, r: (x, y, z + s, c, r) if c else (x + s, y, z, c, r))


def second(s):
    return pairs(lambda x, y, z, c, r: (x + s, y, z, c, r) if c else (x, y, z + s, c, r))


OVER_Y = pairs(lambda x, y, z, c, r: (x, 1 - y, z, c, r))
OVER_CORE = pairs(lambda x, y, z, c, r: (x, y, z, 1 - c, r))
OVER_REP = pairs(lambda x, y, z, c, r: (x, y, z, c, 1 - r))


def send(a, p):
    return lax.ppermute(a, AXES, p)


def gather_parts(mine):
    parts = []
    for rows in (mine, send(mine, OVER_Y)):
        line = jnp.concatenate([rows] + [send(rows, first(-s)) for s in (1, 2, 3)])
        parts += [line] + [send(line, second(-s)) for s in (1, 2, 3)]
    return parts + [send(a, OVER_CORE) for a in parts]


def aggregate_kernel(ids, counts, table, *refs):
    n_parts = NC * NY * NZ
    parts = refs[:n_parts]
    tiles, away, own, panel, live, part_sem, tile_sem = refs[n_parts:]
    blocks, slots = tiles.shape[:2]
    half = blocks // 2
    size = panel.shape[1]
    per_part = (panel.shape[0] - 1) // n_parts
    for n, part in enumerate(parts):
        pltpu.make_async_copy(part, panel.at[pl.ds(n * per_part, per_part)], part_sem.at[n]).start()

    rep = counts[blocks]
    order = [(1 - rep) * half + j for j in range(half)] + [rep * half + j for j in range(half)]

    def groups(b):
        return (counts[b] + (GROUP - 1)) // GROUP

    def copy(b, n, g):
        at = pl.ds(pl.multiple_of(g * GROUP, GROUP), GROUP)
        return pltpu.make_async_copy(tiles.at[b, at], live.at[n, at], tile_sem.at[n])

    for n, b in enumerate(order):

        @pl.loop(0, groups(b))
        def _(g, b=b, n=n):
            copy(b, n, g).start()

    panel[panel.shape[0] - 1] = jnp.zeros(panel.shape[1:], panel.dtype)
    for n, part in enumerate(parts):
        pltpu.make_async_copy(part, panel.at[pl.ds(n * per_part, per_part)], part_sem.at[n]).wait()
    for n, b in enumerate(order):

        @pl.loop(0, groups(b))
        def _(g, b=b, n=n):
            copy(b, n, g).wait()

        def step(g, acc, b=b, n=n):
            for j in range(GROUP):
                k = g * GROUP + j
                at = jnp.where(k < counts[b], table[ids[b, k]], panel.shape[0] - 1)
                acc += jnp.dot(live[n, k], panel[at], preferred_element_type=jnp.float32)
            return acc

        total = lax.fori_loop(0, groups(b), step, jnp.zeros((size, panel.shape[2]), jnp.float32))
        if n < half:
            away[n * size : (n + 1) * size, :] = total.astype(away.dtype)
        else:
            own[(n - half) * size : (n - half + 1) * size, :] = total


def finish_kernel(own, got, weight, bias, gain, out):
    total = own[...] + got[...].astype(jnp.float32)
    high = total.astype(jnp.bfloat16)
    low = (total - high.astype(jnp.float32)).astype(jnp.bfloat16)
    w = weight[...]
    summed = jnp.dot(high, w, preferred_element_type=jnp.float32)
    summed += jnp.dot(low, w, preferred_element_type=jnp.float32)
    hidden = jnp.maximum(summed + bias[...], 0.0)
    centered = hidden - jnp.mean(hidden, axis=1, keepdims=True)
    var = jnp.mean(centered * centered, axis=1, keepdims=True)
    out[...] = (centered / jnp.sqrt(var + 1e-05) * gain[...]).astype(out.dtype)


def per_device(
    features, weight, shift_bias, norm_gain, tile_values, tile_cols, tile_counts, block_order
):
    blocks, _, slots, size, _ = tile_values.shape
    width = features.shape[1]
    held = features.shape[0] // size
    parts = gather_parts(features)

    rep = lax.axis_index("rep")
    x, y, z, core, _ = place(lax.axis_index("rows") * NR)
    order = lax.dynamic_index_in_dim(block_order, rep, 0, keepdims=False)
    sx, sy, sz, score, _ = place(order // held * NR)
    dx, dz = (sx - x) % NX, (sz - z) % NZ
    near, far = jnp.where(score == 0, dx, dz), jnp.where(score == 0, dz, dx)
    table = ((((score ^ core) * NY + (sy ^ y)) * NZ + far) * NX + near) * held + order % held
    counts = jnp.concatenate([tile_counts.reshape(blocks), rep.reshape(1)])

    n_cols = block_order.shape[1]
    smem = pl.BlockSpec(memory_space=pltpu.SMEM)
    anywhere = pl.BlockSpec(memory_space=pl.ANY)
    half_rows = blocks // 2 * size
    away, own = pl.pallas_call(
        aggregate_kernel,
        out_shape=(
            jax.ShapeDtypeStruct((half_rows, width), jnp.bfloat16),
            jax.ShapeDtypeStruct((half_rows, width), jnp.float32),
        ),
        in_specs=[smem] * 3 + [anywhere] * (len(parts) + 1),
        scratch_shapes=[
            pltpu.VMEM((n_cols + 1, size, width), jnp.bfloat16),
            pltpu.VMEM((blocks, slots, size, size), jnp.bfloat16),
            pltpu.SemaphoreType.DMA((len(parts),)),
            pltpu.SemaphoreType.DMA((blocks,)),
        ],
        compiler_params=pltpu.CompilerParams(vmem_limit_bytes=40 << 20),
        name="aggregate",
    )(
        tile_cols.reshape(blocks, slots),
        counts,
        table,
        *[a.reshape(-1, size, width) for a in parts],
        tile_values.reshape(blocks, slots, size, size),
    )
    got = send(away, OVER_REP)
    return pl.pallas_call(
        finish_kernel,
        out_shape=jax.ShapeDtypeStruct((half_rows, weight.shape[1]), jnp.bfloat16),
        name="finish",
    )(own, got, weight, shift_bias.reshape(1, -1), norm_gain.reshape(1, -1))


def solution(mesh):
    in_specs = (
        P(AXES, None),
        P(),
        P(),
        P(),
        P("rows", "rep", None, None, None),
        P("rows", "rep", None),
        P("rows", "rep"),
        P(),
    )
    return jax.shard_map(
        per_device, mesh=mesh, in_specs=in_specs, out_specs=P(AXES, None), check_vma=False
    )
```
